32 devices in a mesh: lon: 4 (over z), head: 4 (over y, core), dp: 2 (over x).
Axes of the slice: x: 2, y: 2, z: 4, core: 2. Of those that a mesh axis runs over, the one named last changes fastest.
Arguments:
- queries: bfloat16 [2, 2048, 3072], P('dp', 'lon', 'head'), may hold values from -6 to 6
- key_heads: bfloat16 [2, 2048, 3072], P('dp', 'lon', 'head'), may hold values from -6 to 6
- value_heads: bfloat16 [2, 2048, 3072], P('dp', 'lon', 'head'), may hold values from -6 to 6
- out_grad: bfloat16 [2, 2048, 3072], P('dp', ('lon', 'head')), may hold values from -6 to 6
- out_weight: bfloat16 [3072, 3072], P('head'), may hold values from -0.109375 to 0.109375
- neighbours: int32 [8, 4], replicated, may hold values from 0 to 7, as said below
- slot_valid: int32 [8, 4], replicated, may hold values 0 or 1
Outputs:
- grad_queries: bfloat16 [2, 2048, 3072], P('dp', 'lon', 'head')
- grad_keys: bfloat16 [2, 2048, 3072], P('dp', 'lon', 'head')
- grad_values: bfloat16 [2, 2048, 3072], P('dp', 'lon', 'head')
- grad_weight: float32 [3072, 3072], P(('lon', 'dp'), 'head')
The draws below stay inside these ranges and needn't reach their ends.
Inputs may be any that keep to these rules, and one draw needn't show every extreme that they name: neighbours[t, j] lies within 2 tiles of t around the closed loop of 8 tiles.
All inputs are finite; a program needn't handle non-finite values.
Results may differ from the reference program's by a relative error of at most 0.012.
The reference program's roundings to bfloat16 on the way (of `weights_low`, `attended`, `grad_attn` and `grad_scores`) count: a program that leaves them out, or rounds other values in their place, can miss the bound.
Values may be sent and summed in bfloat16 or wider, within the bound.
A program may use at most 128 MiB of HBM per device.

```python
import math
import jax
import jax.numpy as jnp
from jax import lax

D = 3072
HEADS = 24
HEAD_DIM = 128
TILE = 256
NB = 4
TOK_DEV = 512
IMAGES = 2
TOKENS = 2048
TILES = 8


def noise_field(key, salt):
    shape = (IMAGES, TOKENS, HEADS * HEAD_DIM)
    drawn = jnp.clip(jax.random.normal(jax.random.fold_in(key, salt), shape, jnp.float32), -5.5, 5.5)
    return drawn


def draw_queries(key, part):
    field = noise_field(key, 11)
    return field.astype(jnp.bfloat16)


def draw_key_heads(key, part):
    field = noise_field(key, 23)
    return field.astype(jnp.bfloat16)


def draw_neighbours(key, part):
    tile_total = TOKENS // TILE
    reach = TOK_DEV // TILE
    offsets = jax.random.randint(jax.random.fold_in(key, 5), (tile_total, NB), -reach, reach + 1)
    return ((jnp.arange(tile_total)[:, None] + offsets) % tile_total).astype(jnp.int32)


def plant(drawn, stream_key, low, largest):
    shape = drawn.shape
    index_at = [jax.random.randint(jax.random.fold_in(stream_key, axis), (), 0, shape[axis]) for axis in range(len(shape))]
    drawn = drawn.at[tuple(index_at)].set(low)
    longest = shape.index(max(shape))
    index_at[longest] = (index_at[longest] + 1) % shape[longest]
    return drawn.at[tuple(index_at)].set(largest)


def strengthened(entries, key, source, target, blocks, factor):
    owner, partner = [(jnp.arange(entries.shape[dim]) // (entries.shape[dim] // blocks)).reshape([-1 if axis == dim else 1 for axis in range(entries.ndim)]) for dim in (source, target)]
    chosen = jax.random.permutation(key, blocks)[partner]
    strong = (owner == chosen) | (owner == (partner + blocks // 2) % blocks)
    return jnp.where(strong, factor * entries, entries)


def block_scale(own_key, shape, pieces, least, largest):
    loudness, own = 1.0, jax.random.fold_in(own_key, 6)
    for axis_at, shards_of in pieces:
        heights = jnp.exp(jax.random.uniform(jax.random.fold_in(own, axis_at), (shards_of,), jnp.float32, least / len(pieces), largest / len(pieces)))
        loudness = loudness * jnp.repeat(heights, shape[axis_at] // shards_of).reshape([-1 if axis == axis_at else 1 for axis in range(len(shape))])
    return loudness


def centred(rng, shape, deviation, most, pieces=(), kind=jnp.bfloat16):
    array = jax.random.normal(rng, shape, jnp.float32) * deviation
    if len(pieces) > 0:
        array = block_scale(rng, shape, pieces, -0.22, 0.18) * array
    return jnp.clip(array, min=-most, max=most).astype(kind)


def bell_draw_with(key, shape, scale, bound, cuts, heavy, kind=jnp.bfloat16):
    array = scale * jax.random.normal(key, shape, jnp.float32)
    if cuts:
        array = array * block_scale(key, shape, cuts, -0.22, 0.18)
    return jnp.clip(strengthened(array, jax.random.fold_in(key, 3), *heavy), -bound, bound).astype(kind)


def setup_inputs(seed: int = 0) -> dict:
    key_of = jax.random.split(jax.random.key(seed), 8)
    return {
        "queries": draw_queries(jax.random.fold_in(key_of[7], 71), 0),
        "key_heads": draw_key_heads(jax.random.fold_in(key_of[7], 71), 0),
        "value_heads": centred(key_of[2], (IMAGES, TOKENS, HEADS * HEAD_DIM), 1.0, 6.0, ((0, 2), (1, 4), (2, 4))),
        "out_grad": bell_draw_with(key_of[3], (IMAGES, TOKENS, D), 1.0, 6.0, ((0, 2), (1, 16)), (1, 2, 16, 2.0)),
        "out_weight": centred(key_of[4], (HEADS * HEAD_DIM, D), (HEADS * HEAD_DIM) ** -0.5, 0.109375, ((0, 4),)),
        "neighbours": draw_neighbours(jax.random.fold_in(key_of[7], 71), 0),
        "slot_valid": plant((jax.random.randint(key_of[6], (TILES, NB), 0, 4) < 3).astype(jnp.int32), jax.random.fold_in(key_of[6], 1), 0, 1),
    }


def attend_head(query_tiles, key_tiles, value_tiles, grad_tiles, slot_tiles, slot_live):
    factor = 1.0 / math.sqrt(HEAD_DIM)
    picked_keys = key_tiles[slot_tiles].astype(jnp.float32)
    picked_values = value_tiles[slot_tiles].astype(jnp.float32)
    query_wide = query_tiles.astype(jnp.float32)
    grad_wide = grad_tiles.astype(jnp.float32)
    scores = jnp.einsum('qid,qsjd->qisj', query_wide, picked_keys) * factor
    is_live = (slot_live > 0)[:, None, :, None]
    scores = jnp.where(is_live, scores, -jnp.inf)
    row_max = lax.optimization_barrier(jnp.max(scores, axis=(2, 3), keepdims=True))
    raised = jnp.exp(scores - row_max)
    weights = raised / lax.optimization_barrier(jnp.sum(raised, axis=(2, 3), keepdims=True))
    weights_low = weights.astype(jnp.bfloat16)
    low_wide = weights_low.astype(jnp.float32)
    attended = jnp.einsum('qisj,qsjd->qid', low_wide, picked_values).astype(jnp.bfloat16)
    row_delta = lax.optimization_barrier(jnp.sum(grad_wide * attended.astype(jnp.float32), axis=-1))
    grad_weights = jnp.einsum('qid,qsjd->qisj', grad_wide, picked_values)
    grad_scores = (weights * (grad_weights - row_delta[:, :, None, None]) * factor).astype(jnp.bfloat16)
    scores_wide = grad_scores.astype(jnp.float32)
    grad_query = jnp.einsum('qisj,qsjd->qid', scores_wide, picked_keys).astype(jnp.bfloat16)
    key_blocks = jnp.einsum('qisj,qid->qsjd', scores_wide, query_wide)
    value_blocks = jnp.einsum('qisj,qid->qsjd', low_wide, grad_wide)
    key_sums = jnp.zeros(key_tiles.shape, jnp.float32).at[slot_tiles].add(key_blocks)
    value_sums = jnp.zeros(value_tiles.shape, jnp.float32).at[slot_tiles].add(value_blocks)
    return (attended, grad_query, key_sums.astype(jnp.bfloat16), value_sums.astype(jnp.bfloat16))

def heads_first(matrix):
    return matrix.reshape(TILES, TILE, HEADS, HEAD_DIM).transpose(2, 0, 1, 3)

def tokens_first(blocks):
    return blocks.transpose(1, 2, 0, 3).reshape(TOKENS, HEADS * HEAD_DIM)

def reference(queries, key_heads, value_heads, out_grad, out_weight, neighbours, slot_valid):
    slot_tiles = jnp.concatenate([jnp.arange(TILES, dtype=jnp.int32)[:, None], neighbours.astype(jnp.int32)], axis=1)
    slot_live = jnp.concatenate([jnp.ones((TILES, 1), jnp.int32), slot_valid.astype(jnp.int32)], axis=1)

    def one_image(running, inputs):
        query_rows, key_rows, value_rows, grad_rows = inputs
        grad_attn = jnp.dot(grad_rows, out_weight.T, preferred_element_type=jnp.float32).astype(jnp.bfloat16)

        def per_head(head_parts):
            return attend_head(head_parts[0], head_parts[1], head_parts[2], head_parts[3], slot_tiles, slot_live)
        attended, grad_query, grad_key, grad_value = lax.map(per_head, (heads_first(query_rows), heads_first(key_rows), heads_first(value_rows), heads_first(grad_attn)))
        attn_out = tokens_first(attended)
        running = running + jnp.dot(grad_rows.T, attn_out, preferred_element_type=jnp.float32)
        return (running, (tokens_first(grad_query), tokens_first(grad_key), tokens_first(grad_value)))
    zero_grad = jnp.zeros((D, HEADS * HEAD_DIM), jnp.float32)
    grad_weight, stacked = lax.scan(one_image, zero_grad, (queries, key_heads, value_heads, out_grad))
    return (stacked[0], stacked[1], stacked[2], grad_weight)
```

```python
import functools
import math

import jax
import jax.numpy as jnp
from jax import lax
from jax.experimental import pallas as pl
from jax.experimental.pallas import tpu as pltpu
from jax.sharding import PartitionSpec as P

HEAD_DIM = 128
TILE = 256
REACH = 2
CHUNK_HEADS = 2
NT = (((1,), (1,)), ((), ()))
NN = (((1,), (0,)), ((), ()))
TN = (((0,), (0,)), ((), ()))


def mul(a, b, dims):
    return lax.dot_general(a, b, dims, preferred_element_type=jnp.float32)


def shifted(value, axis, steps):
    count = lax.axis_size(axis)
    pairs = [(source, (source + steps) % count) for source in range(count)]
    return lax.ppermute(value, axis, pairs)


def flipped(value, axis, bit):
    count = lax.axis_size(axis)
    return lax.ppermute(value, axis, [(source, source ^ bit) for source in range(count)])


def attend_kernel(
    counts_ref,
    q_ref,
    k_ref,
    v_ref,
    g_ref,
    behind_ref,
    beyond_ref,
    dq_ref,
    att_ref,
    own_ref,
    to_behind_ref,
    to_beyond_ref,
    k_ext,
    v_ext,
    dk_ext,
    dv_ext,
):
    factor = 1.0 / math.sqrt(HEAD_DIM)
    rows = q_ref.shape[0]
    tiles = rows // TILE
    k_ext[0:rows] = behind_ref[0]
    k_ext[rows : 2 * rows] = k_ref[...]
    k_ext[2 * rows : 3 * rows] = beyond_ref[0]
    v_ext[0:rows] = behind_ref[1]
    v_ext[rows : 2 * rows] = v_ref[...]
    v_ext[2 * rows : 3 * rows] = beyond_ref[1]
    wide = 2 * REACH + 1
    seen = set()
    for i in range(tiles):
        here = slice(i * TILE, (i + 1) * TILE)
        q = q_ref[here]
        g = g_ref[here]
        spots = []
        for o in range(wide):
            at = (i + tiles - REACH + o) * TILE
            spots.append(slice(at, at + TILE))
        live = [counts_ref[i * wide + o] for o in range(wide)]
        scores = []
        top = None
        for o in range(wide):
            bias = jnp.where(live[o] > 0.0, 0.0, -jnp.inf)
            s = mul(k_ext[spots[o]], q, NT) * factor + bias
            scores.append(s)
            m = jnp.max(s, axis=0, keepdims=True)
            top = m if top is None else jnp.maximum(top, m)
        total = None
        raised = []
        for o in range(wide):
            e = jnp.exp(scores[o] - top)
            raised.append(e)
            part = jnp.sum(e, axis=0, keepdims=True) * live[o]
            total = part if total is None else total + part
        inverse = 1.0 / total
        weights = []
        att = None
        for o in range(wide):
            w = raised[o] * inverse
            weights.append(w)
            low = w.astype(jnp.bfloat16)
            part = mul(v_ext[spots[o]], low, TN) * live[o]
            att = part if att is None else att + part
            dv = mul(low, g, NN) * live[o]
            if spots[o].start in seen:
                dv_ext[spots[o]] += dv
            else:
                dv_ext[spots[o]] = dv
        att_rows = att.T.astype(jnp.bfloat16)
        att_ref[here] = att_rows
        g_turned = g.astype(jnp.float32).T
        delta = jnp.sum(
            g_turned * att.astype(jnp.bfloat16).astype(jnp.float32), axis=0, keepdims=True
        )
        dq = None
        for o in range(wide):
            dw = mul(v_ext[spots[o]], g, NT)
            ds = (weights[o] * (dw - delta) * factor).astype(jnp.bfloat16)
            part = mul(k_ext[spots[o]], ds, TN) * live[o]
            dq = part if dq is None else dq + part
            dk = mul(ds, q, NN) * live[o]
            if spots[o].start in seen:
                dk_ext[spots[o]] += dk
            else:
                dk_ext[spots[o]] = dk
            seen.add(spots[o].start)
        dq_ref[here] = dq.T.astype(jnp.bfloat16)
    for n, ext in ((0, dk_ext), (1, dv_ext)):
        to_behind_ref[n] = ext[0:rows].astype(jnp.bfloat16)
        own_ref[n] = ext[rows : 2 * rows]
        to_beyond_ref[n] = ext[2 * rows : 3 * rows].astype(jnp.bfloat16)


def attend(counts, q, k, v, g, behind, beyond, first_head, heads):
    rows = q.shape[0]
    cols = heads * HEAD_DIM
    whole = pl.BlockSpec((rows, HEAD_DIM), lambda h: (0, first_head + h))
    part = pl.BlockSpec((rows, HEAD_DIM), lambda h: (0, h))
    pair = pl.BlockSpec((2, rows, HEAD_DIM), lambda h: (0, 0, h))
    flops = 12 * rows * (2 * REACH + 1) * TILE * cols
    return pl.pallas_call(
        attend_kernel,
        grid=(heads,),
        in_specs=[
            pl.BlockSpec(memory_space=pltpu.SMEM),
            whole,
            whole,
            whole,
            whole,
            pair,
            pair,
        ],
        out_specs=[part, part, pair, pair, pair],
        out_shape=[
            jax.ShapeDtypeStruct((rows, cols), jnp.bfloat16),
            jax.ShapeDtypeStruct((rows, cols), jnp.bfloat16),
            jax.ShapeDtypeStruct((2, rows, cols), jnp.float32),
            jax.ShapeDtypeStruct((2, rows, cols), jnp.bfloat16),
            jax.ShapeDtypeStruct((2, rows, cols), jnp.bfloat16),
        ],
        scratch_shapes=[
            pltpu.VMEM((3 * rows, HEAD_DIM), jnp.bfloat16),
            pltpu.VMEM((3 * rows, HEAD_DIM), jnp.bfloat16),
            pltpu.VMEM((3 * rows, HEAD_DIM), jnp.float32),
            pltpu.VMEM((3 * rows, HEAD_DIM), jnp.float32),
        ],
        cost_estimate=pl.CostEstimate(
            flops=flops, bytes_accessed=20 * rows * cols * 2, transcendentals=rows * 1280 * heads
        ),
    )(counts, q, k, v, g, behind, beyond)


def halved(blocks, axis, dim):
    count = lax.axis_size(axis)
    me = lax.axis_index(axis)
    bit = 1
    while bit < count:
        mine = (me // bit) % 2
        shape = blocks.shape
        split = shape[:dim] + (shape[dim] // 2, 2) + shape[dim + 1 :]
        paired = blocks.reshape(split)
        kept = lax.dynamic_index_in_dim(paired, mine, dim + 1, keepdims=False)
        sent = lax.dynamic_index_in_dim(paired, 1 - mine, dim + 1, keepdims=False)
        arrived = flipped(sent.astype(jnp.bfloat16), axis, bit)
        blocks = kept + arrived.astype(jnp.float32)
        bit *= 2
    return blocks


def local(queries, key_heads, value_heads, out_grad, out_weight, neighbours, slot_valid):
    q, k, v = queries[0], key_heads[0], value_heads[0]
    rows, features = q.shape
    heads = features // HEAD_DIM
    tiles = rows // TILE
    lon_count = lax.axis_size("lon")
    dp_count = lax.axis_size("dp")
    head_count = lax.axis_size("head")
    tile_total = tiles * lon_count
    first_tile = lax.axis_index("lon") * tiles
    own_rows = lax.dynamic_slice_in_dim(neighbours, first_tile, tiles, 0)
    own_live = lax.dynamic_slice_in_dim(slot_valid, first_tile, tiles, 0)
    index = first_tile + jnp.arange(tiles, dtype=jnp.int32)
    offset = (own_rows - index[:, None] + REACH + tile_total) % tile_total
    span = jnp.arange(2 * REACH + 1, dtype=jnp.int32)
    named = (offset[:, :, None] == span) & (own_live > 0)[:, :, None]
    counts = jnp.sum(named.astype(jnp.float32), axis=1) + (span == REACH).astype(jnp.float32)
    counts = counts.reshape(-1)

    chunks = heads // CHUNK_HEADS
    cols = CHUNK_HEADS * HEAD_DIM
    behind, beyond = [], []
    for c in range(chunks):
        cut = slice(c * cols, (c + 1) * cols)
        stacked = jnp.stack((k[:, cut], v[:, cut]))
        behind.append(shifted(stacked, "lon", 1))
        beyond.append(shifted(stacked, "lon", -1))

    mine = out_grad[0]
    got = {0: mine}
    bit = head_count // 2
    while bit:
        for at in sorted(got):
            got[at ^ bit] = flipped(got[at], "head", bit)
        bit //= 2
    piece = mine.shape[0]
    me = lax.axis_index("head")
    grad_rows = jnp.zeros((rows, mine.shape[1]), mine.dtype)
    for at in sorted(got):
        grad_rows = lax.dynamic_update_slice_in_dim(grad_rows, got[at], (me ^ at) * piece, 0)
    grad_attn = mul(grad_rows, out_weight, NT).astype(jnp.bfloat16)

    dq, summed, grad_weight = [], [], []
    for c in range(chunks):
        part_q, att, own, to_behind, to_beyond = attend(
            counts, q, k, v, grad_attn, behind[c], beyond[c], c * CHUNK_HEADS, CHUNK_HEADS
        )
        dq.append(part_q)
        from_beyond = shifted(to_behind, "lon", -1)
        from_behind = shifted(to_beyond, "lon", 1)
        summed.append(
            (own + from_beyond.astype(jnp.float32) + from_behind.astype(jnp.float32)).astype(
                jnp.bfloat16
            )
        )
        term = mul(grad_rows, att, TN)
        blocks = term.reshape(lon_count, dp_count, -1, cols)
        blocks = halved(blocks, "dp", 1)
        blocks = halved(blocks, "lon", 0)
        grad_weight.append(blocks[0, 0])
    joined = jnp.concatenate(summed, axis=2)
    return (
        jnp.concatenate(dq, axis=1)[None],
        joined[0][None],
        joined[1][None],
        jnp.concatenate(grad_weight, axis=1),
    )


def solution(mesh):
    in_specs = (
        P("dp", "lon", "head"),
        P("dp", "lon", "head"),
        P("dp", "lon", "head"),
        P("dp", ("lon", "head"), None),
        P("head", None),
        P(),
        P(),
    )
    out_specs = (
        P("dp", "lon", "head"),
        P("dp", "lon", "head"),
        P("dp", "lon", "head"),
        P(("lon", "dp"), "head"),
    )
    return jax.shard_map(local, mesh=mesh, in_specs=in_specs, out_specs=out_specs, check_vma=False)
```

```python
import functools
import math

import jax
import jax.numpy as jnp
from jax import lax
from jax.experimental import pallas as pl
from jax.experimental.pallas import tpu as pltpu
from jax.sharding import PartitionSpec as P

HEAD_DIM = 128
TILE = 256
REACH = 2
WIDE = 2 * REACH + 1
CHUNK_HEADS = 2
BLOCK = 256
NT = (((1,), (1,)), ((), ()))
NN = (((1,), (0,)), ((), ()))
TN = (((0,), (0,)), ((), ()))
MESH = pl.DeviceIdType.MESH


def mul(a, b, dims):
    return lax.dot_general(a, b, dims, preferred_element_type=jnp.float32)


def columns(start, size):
    return pl.ds(pl.multiple_of(start, HEAD_DIM), size)


def attend_head(col, att_col, counts_ref, refs):
    factor = 1.0 / math.sqrt(HEAD_DIM)
    q_s, k_s, v_s, ga, kv_in, dq_ref, att_s, own, dsend, ext = refs
    rows = q_s.shape[0]
    tiles = rows // TILE
    lanes = columns(col, HEAD_DIM)

    def tile_of(n, j):
        part, at = divmod(j, tiles)
        here = slice(at * TILE, (at + 1) * TILE)
        if part == 1:
            return (k_s, v_s)[n][here, lanes]
        return kv_in[part // 2, n, here, lanes]

    seen = set()
    for i in range(tiles):
        here = slice(i * TILE, (i + 1) * TILE)
        q = q_s[here, lanes]
        g = ga[here, lanes]
        spots = [i + tiles - REACH + o for o in range(WIDE)]
        live = [counts_ref[i * WIDE + o] for o in range(WIDE)]
        scores = []
        top = None
        for o in range(WIDE):
            bias = jnp.where(live[o] > 0.0, 0.0, -jnp.inf)
            s = mul(tile_of(0, spots[o]), q, NT) * factor + bias
            scores.append(s)
            m = jnp.max(s, axis=0, keepdims=True)
            top = m if top is None else jnp.maximum(top, m)
        total = None
        raised = []
        for o in range(WIDE):
            e = jnp.exp(scores[o] - top)
            raised.append(e)
            part = jnp.sum(e, axis=0, keepdims=True) * live[o]
            total = part if total is None else total + part
        inverse = 1.0 / total
        weights = []
        att = None
        for o in range(WIDE):
            w = raised[o] * inverse
            weights.append(w)
            low = w.astype(jnp.bfloat16)
            part = mul(tile_of(1, spots[o]), low, TN) * live[o]
            att = part if att is None else att + part
            dv = mul(low, g, NN) * live[o]
            spot = slice(spots[o] * TILE, (spots[o] + 1) * TILE)
            if spots[o] in seen:
                ext[1, spot] += dv
            else:
                ext[1, spot] = dv
        att_s[here, columns(att_col, HEAD_DIM)] = att.T.astype(jnp.bfloat16)
        g_turned = g.astype(jnp.float32).T
        delta = jnp.sum(
            g_turned * att.astype(jnp.bfloat16).astype(jnp.float32), axis=0, keepdims=True
        )
        dq = None
        for o in range(WIDE):
            dw = mul(tile_of(1, spots[o]), g, NT)
            ds = (weights[o] * (dw - delta) * factor).astype(jnp.bfloat16)
            part = mul(tile_of(0, spots[o]), ds, TN) * live[o]
            dq = part if dq is None else dq + part
            dk = mul(ds, q, NN) * live[o]
            spot = slice(spots[o] * TILE, (spots[o] + 1) * TILE)
            if spots[o] in seen:
                ext[0, spot] += dk
            else:
                ext[0, spot] = dk
            seen.add(spots[o])
        dq_ref[here, lanes] = dq.T.astype(jnp.bfloat16)
    for n in range(2):
        dsend[0, n, :, lanes] = ext[n, 0:rows].astype(jnp.bfloat16)
        own[n, :, lanes] = ext[n, rows : 2 * rows]
        dsend[1, n, :, lanes] = ext[n, 2 * rows : 3 * rows].astype(jnp.bfloat16)


def kernel(
    sizes,
    counts_ref,
    q_ref,
    k_ref,
    v_ref,
    og_ref,
    w_ref,
    dq_ref,
    dk_ref,
    dv_ref,
    gw_ref,
    q_s,
    k_s,
    v_s,
    w_s,
    og_s,
    og_t,
    ga,
    kv_in,
    ext,
    own,
    dsend,
    drecv,
    att_s,
    gw_s,
    acc,
    wsend,
    wrecv,
    local_sem,
    kv_ss,
    kv_rs,
    og_ss,
    og_rs,
    d_ss,
    d_rs,
    w_ss,
    w_rs,
):
    lon_count, head_count, dp_count = sizes
    rows, features = q_s.shape
    model = og_s.shape[1]
    piece = og_ref.shape[0]
    cols = CHUNK_HEADS * HEAD_DIM
    chunks = features // cols
    lon = lax.axis_index("lon")
    head = lax.axis_index("head")
    dp = lax.axis_index("dp")
    after = {"lon": lax.rem(lon + 1, lon_count)}
    before = {"lon": lax.rem(lon + lon_count - 1, lon_count)}

    def partner(axis, me, bit):
        low = lax.rem(me // bit, 2)
        return {axis: me + bit - 2 * bit * low}, low

    stages = []
    for axis, me, count in (("dp", dp, dp_count), ("lon", lon, lon_count)):
        bit = 1
        while bit < count:
            stages.append(partner(axis, me, bit))
            bit *= 2
    gathers = []
    held = [0]
    bit = head_count // 2
    while bit:
        for at in list(held):
            gathers.append((bit, at))
            held.append(at + bit)
        bit //= 2

    greeted = [after, before] + [there for there, _ in stages]
    bit = head_count // 2
    while bit:
        greeted.append(partner("head", head, bit)[0])
        bit //= 2
    barrier = pltpu.get_barrier_semaphore()
    for there in greeted:
        pl.semaphore_signal(barrier, inc=1, device_id=there, device_id_type=MESH)
    pl.semaphore_wait(barrier, len(greeted))

    def remote(src, dst, ss, rs, there):
        return pltpu.make_async_remote_copy(
            src_ref=src, dst_ref=dst, send_sem=ss, recv_sem=rs, device_id=there, device_id_type=MESH
        )

    def piece_at(offset):
        at = 0
        bit = 1
        while bit < head_count:
            low = lax.rem(head // bit, 2)
            at = at + bit * ((1 - low) if offset & bit else low)
            bit *= 2
        return pl.ds(pl.multiple_of(at * piece, piece), piece)

    kv_copies = []
    d_copies = []
    for c in range(chunks):
        cut = slice(c * cols, (c + 1) * cols)
        some, others = [], []
        for n, ref in ((0, k_ref), (1, v_ref)):
            for way, there in ((0, after), (1, before)):
                at = (c * 2 + n) * 2 + way
                some.append(
                    remote(
                        ref.at[:, cut], kv_in.at[way, n, :, cut], kv_ss.at[at], kv_rs.at[at], there
                    )
                )
            for way, there in ((0, before), (1, after)):
                at = (c * 2 + n) * 2 + way
                others.append(
                    remote(
                        dsend.at[way, n, :, cut],
                        drecv.at[way, n, :, cut],
                        d_ss.at[at],
                        d_rs.at[at],
                        there,
                    )
                )
        kv_copies.append(some)
        d_copies.append(others)

    og_copies = []
    for at, (bit, offset) in enumerate(gathers):
        src = og_ref if offset == 0 else og_s.at[piece_at(offset)]
        og_copies.append(
            remote(
                src,
                og_s.at[piece_at(offset)],
                og_ss.at[at],
                og_rs.at[at],
                partner("head", head, bit)[0],
            )
        )
    for copy in kv_copies[0]:
        copy.start()
    for copy, (bit, offset) in zip(og_copies, gathers):
        if offset == 0:
            copy.start()
    for some in kv_copies[1:]:
        for copy in some:
            copy.start()
    local_copies = [
        pltpu.make_async_copy(src, dst, local_sem.at[at])
        for at, (src, dst) in enumerate(
            (
                (og_ref, og_s.at[piece_at(0)]),
                (w_ref, w_s),
                (q_ref, q_s),
                (k_ref, k_s),
                (v_ref, v_s),
            )
        )
    ]
    for copy in local_copies:
        copy.start()
    where = {}
    for at, (bit, offset) in enumerate(gathers):
        where[bit + offset] = at
    arrived = set()
    for copy, (bit, offset) in zip(og_copies, gathers):
        if offset:
            og_copies[where[offset]].wait_recv()
            arrived.add(where[offset])
            copy.start()
    for at, copy in enumerate(og_copies):
        if at not in arrived:
            copy.wait_recv()
    for copy in local_copies:
        copy.wait()

    @pl.loop(0, chunks)
    def _(c):
        ga[:, columns(c * cols, cols)] = mul(
            og_s[...], w_s[pl.ds(pl.multiple_of(c * cols, cols), cols)], NT
        ).astype(jnp.bfloat16)

    @pl.loop(0, model // BLOCK)
    def _(b):
        og_t[pl.ds(pl.multiple_of(b * BLOCK, BLOCK), BLOCK)] = og_s[:, columns(b * BLOCK, BLOCK)].T

    shares = lon_count * dp_count
    share = model // shares
    last = len(stages)
    sent_counts = [shares >> (s + 1) for s in range(last)]
    starts = [sum(sent_counts[:s]) for s in range(last)]

    def weight_copy(s, c):
        span = pl.ds(starts[s], sent_counts[s])
        at = c * last + s
        return remote(
            wsend.at[c, span], wrecv.at[c, span], w_ss.at[at], w_rs.at[at], stages[s][0]
        )

    def share_rows(b):
        return pl.ds(pl.multiple_of(b * share, 16), share)

    def stage(s, c):
        if s > 0:
            weight_copy(s - 1, c).wait_recv()

            @pl.loop(0, sent_counts[s - 1])
            def _(j):
                acc[c, j] += wrecv[c, starts[s - 1] + j].astype(jnp.float32)

        if s == last:
            gw_ref[:, c * cols : (c + 1) * cols] = acc[c, 0]
            return
        mine = stages[s][1]

        @pl.loop(0, sent_counts[s])
        def _(j):
            if s == 0:
                gone = gw_s[share_rows(2 * j + 1 - mine)]
                kept = gw_s[share_rows(2 * j + mine)]
            else:
                gone = acc[c, 2 * j + 1 - mine]
                kept = acc[c, 2 * j + mine]
            wsend[c, starts[s] + j] = gone.astype(jnp.bfloat16)
            acc[c, j] = kept

        weight_copy(s, c).start()

    refs = (q_s, k_s, v_s, ga, kv_in, dq_ref, att_s, own, dsend, ext)
    for c in range(chunks):
        for copy in kv_copies[c]:
            copy.wait_recv()

        @pl.loop(0, CHUNK_HEADS)
        def _(h):
            attend_head(c * cols + h * HEAD_DIM, h * HEAD_DIM, counts_ref, refs)

        for copy in d_copies[c]:
            copy.start()

        @pl.loop(0, model // BLOCK)
        def _(b):
            span = pl.ds(pl.multiple_of(b * BLOCK, BLOCK), BLOCK)
            gw_s[span] = mul(og_t[span], att_s[...], NN)

        stage(0, c)
        if c > 0:
            stage(1, c - 1)
    stage(1, chunks - 1)
    for s in range(2, last + 1):
        for c in range(chunks):
            if s == 2:
                cut = slice(c * cols, (c + 1) * cols)
                for copy in d_copies[c]:
                    copy.wait_recv()
                for n, ref in ((0, dk_ref), (1, dv_ref)):
                    ref[:, cut] = (
                        own[n, :, cut]
                        + drecv[0, n, :, cut].astype(jnp.float32)
                        + drecv[1, n, :, cut].astype(jnp.float32)
                    ).astype(jnp.bfloat16)
            stage(s, c)
    for copy in og_copies:
        copy.wait_send()
    for c in range(chunks):
        for copy in kv_copies[c] + d_copies[c]:
            copy.wait_send()
        for s in range(last):
            weight_copy(s, c).wait_send()


def local(queries, key_heads, value_heads, out_grad, out_weight, neighbours, slot_valid):
    q, k, v = queries[0], key_heads[0], value_heads[0]
    rows, features = q.shape
    tiles = rows // TILE
    sizes = tuple(lax.axis_size(axis) for axis in ("lon", "head", "dp"))
    lon_count, head_count, dp_count = sizes
    tile_total = tiles * lon_count
    first_tile = lax.axis_index("lon") * tiles
    own_rows = lax.dynamic_slice_in_dim(neighbours, first_tile, tiles, 0)
    own_live = lax.dynamic_slice_in_dim(slot_valid, first_tile, tiles, 0)
    index = first_tile + jnp.arange(tiles, dtype=jnp.int32)
    offset = (own_rows - index[:, None] + REACH + tile_total) % tile_total
    span = jnp.arange(WIDE, dtype=jnp.int32)
    named = (offset[:, :, None] == span) & (own_live > 0)[:, :, None]
    counts = jnp.sum(named.astype(jnp.float32), axis=1) + (span == REACH).astype(jnp.float32)
    counts = counts.reshape(-1)

    model = out_weight.shape[1]
    cols = CHUNK_HEADS * HEAD_DIM
    chunks = features // cols
    shares = lon_count * dp_count
    share = model // shares
    bits = shares.bit_length() - 1
    low, wide = jnp.bfloat16, jnp.float32
    vmem = pltpu.VMEM
    dma = pltpu.SemaphoreType.DMA
    dq, dk, dv, gw = pl.pallas_call(
        functools.partial(kernel, sizes),
        out_shape=[
            jax.ShapeDtypeStruct((rows, features), low),
            jax.ShapeDtypeStruct((rows, features), low),
            jax.ShapeDtypeStruct((rows, features), low),
            jax.ShapeDtypeStruct((share, features), wide),
        ],
        in_specs=[pl.BlockSpec(memory_space=pltpu.SMEM)]
        + [pl.BlockSpec(memory_space=pl.ANY)] * 5,
        out_specs=[pl.BlockSpec(memory_space=vmem)] * 4,
        scratch_shapes=[
            vmem((rows, features), low),
            vmem((rows, features), low),
            vmem((rows, features), low),
            vmem((features, model), low),
            vmem((rows, model), low),
            vmem((model, rows), low),
            vmem((rows, features), low),
            vmem((2, 2, rows, features), low),
            vmem((2, 3 * rows, HEAD_DIM), wide),
            vmem((2, rows, features), wide),
            vmem((2, 2, rows, features), low),
            vmem((2, 2, rows, features), low),
            vmem((rows, cols), low),
            vmem((model, cols), wide),
            vmem((chunks, shares // 2, share, cols), wide),
            vmem((chunks, shares - 1, share, cols), low),
            vmem((chunks, shares - 1, share, cols), low),
            dma((5,)),
            dma((chunks * 4,)),
            dma((chunks * 4,)),
            dma((head_count - 1,)),
            dma((head_count - 1,)),
            dma((chunks * 4,)),
            dma((chunks * 4,)),
            dma((chunks * bits,)),
            dma((chunks * bits,)),
        ],
        compiler_params=pltpu.CompilerParams(
            collective_id=0, has_side_effects=True, vmem_limit_bytes=60 * 1024 * 1024
        ),
    )(counts, q, k, v, out_grad[0], out_weight)
    return (dq[None], dk[None], dv[None], gw)


def solution(mesh):
    in_specs = (
        P("dp", "lon", "head"),
        P("dp", "lon", "head"),
        P("dp", "lon", "head"),
        P("dp", ("lon", "head"), None),
        P("head", None),
        P(),
        P(),
    )
    out_specs = (
        P("dp", "lon", "head"),
        P("dp", "lon", "head"),
        P("dp", "lon", "head"),
        P(("lon", "dp"), "head"),
    )
    return jax.shard_map(local, mesh=mesh, in_specs=in_specs, out_specs=out_specs, check_vma=False)
```

```python
import functools
import math

import jax
import jax.numpy as jnp
from jax import lax
from jax.experimental import pallas as pl
from jax.experimental.pallas import tpu as pltpu
from jax.sharding import PartitionSpec as P

HEAD_DIM = 128
TILE = 256
REACH = 2
WIDE = 2 * REACH + 1
CHUNK_HEADS = 2
BLOCK = 256
NT = (((1,), (1,)), ((), ()))
NN = (((1,), (0,)), ((), ()))
TN = (((0,), (0,)), ((), ()))
MESH = pl.DeviceIdType.MESH


def mul(a, b, dims):
    return lax.dot_general(a, b, dims, preferred_element_type=jnp.float32)


def columns(start, size):
    return pl.ds(pl.multiple_of(start, HEAD_DIM), size)


def attend_head(col, att_col, counts, refs):
    factor = 1.0 / math.sqrt(HEAD_DIM)
    q_s, k_s, v_s, ga, kv_in, dq_ref, att_s, own, dsend, ext = refs
    rows = q_s.shape[0]
    tiles = rows // TILE
    lanes = columns(col, HEAD_DIM)

    def tile_of(n, j):
        part, at = divmod(j, tiles)
        here = slice(at * TILE, (at + 1) * TILE)
        if part == 1:
            return (k_s, v_s)[n][here, lanes]
        return kv_in[part // 2, n, here, lanes]

    seen = set()
    for i in range(tiles):
        here = slice(i * TILE, (i + 1) * TILE)
        q = q_s[here, lanes]
        g = ga[here, lanes]
        spots = [i + tiles - REACH + o for o in range(WIDE)]
        live = counts[i]
        scores = []
        top = None
        for o in range(WIDE):
            bias = jnp.where(live[o] > 0.0, 0.0, -jnp.inf)
            s = mul(tile_of(0, spots[o]), q, NT) * factor + bias
            scores.append(s)
            m = jnp.max(s, axis=0, keepdims=True)
            top = m if top is None else jnp.maximum(top, m)
        total = None
        raised = []
        for o in range(WIDE):
            e = jnp.exp(scores[o] - top)
            raised.append(e)
            part = jnp.sum(e, axis=0, keepdims=True) * live[o]
            total = part if total is None else total + part
        inverse = 1.0 / total
        weights = []
        att = None
        for o in range(WIDE):
            w = raised[o] * inverse
            weights.append(w)
            low = w.astype(jnp.bfloat16)
            part = mul(tile_of(1, spots[o]), low, TN) * live[o]
            att = part if att is None else att + part
            dv = mul(low, g, NN) * live[o]
            spot = slice(spots[o] * TILE, (spots[o] + 1) * TILE)
            if spots[o] in seen:
                ext[1, spot] += dv
            else:
                ext[1, spot] = dv
        att_s[here, columns(att_col, HEAD_DIM)] = att.T.astype(jnp.bfloat16)
        g_turned = g.astype(jnp.float32).T
        delta = jnp.sum(
            g_turned * att.astype(jnp.bfloat16).astype(jnp.float32), axis=0, keepdims=True
        )
        dq = None
        for o in range(WIDE):
            dw = mul(tile_of(1, spots[o]), g, NT)
            ds = (weights[o] * (dw - delta) * factor).astype(jnp.bfloat16)
            part = mul(tile_of(0, spots[o]), ds, TN) * live[o]
            dq = part if dq is None else dq + part
            dk = mul(ds, q, NN) * live[o]
            spot = slice(spots[o] * TILE, (spots[o] + 1) * TILE)
            if spots[o] in seen:
                ext[0, spot] += dk
            else:
                ext[0, spot] = dk
            seen.add(spots[o])
        dq_ref[here, lanes] = dq.T.astype(jnp.bfloat16)
    for n in range(2):
        dsend[0, n, :, lanes] = ext[n, 0:rows].astype(jnp.bfloat16)
        own[n, :, lanes] = ext[n, rows : 2 * rows]
        dsend[1, n, :, lanes] = ext[n, 2 * rows : 3 * rows].astype(jnp.bfloat16)


def kernel(
    sizes,
    near_ref,
    valid_ref,
    q_ref,
    k_ref,
    v_ref,
    og_ref,
    w_ref,
    dq_ref,
    dk_ref,
    dv_ref,
    gw_ref,
    q_s,
    k_s,
    v_s,
    w_s,
    og_s,
    og_t,
    ga,
    kv_in,
    ext,
    own,
    dsend,
    drecv,
    att_s,
    gw_s,
    acc,
    wsend,
    wrecv,
    local_sem,
    kv_ss,
    kv_rs,
    og_ss,
    og_rs,
    d_ss,
    d_rs,
    w_ss,
    w_rs,
    relay_ss,
    lsend,
    lrecv,
    l_ss,
    l_rs,
):
    lon_count, head_count, dp_count = sizes
    rows, features = q_s.shape
    model = og_s.shape[1]
    piece = og_ref.shape[0]
    cols = CHUNK_HEADS * HEAD_DIM
    chunks = features // cols
    lon = lax.axis_index("lon")
    head = lax.axis_index("head")
    dp = lax.axis_index("dp")
    line = lon_count == 4
    tiles = rows // TILE
    counts = []
    for i in range(tiles):
        tile = lon * tiles + i
        live = [jnp.float32(1.0 if o == REACH else 0.0) for o in range(WIDE)]
        for j in range(near_ref.shape[1]):
            away = lax.rem(near_ref[tile, j] - tile + REACH + tiles * lon_count, tiles * lon_count)
            used = jnp.where(valid_ref[tile, j] > 0, 1.0, 0.0)
            live = [live[o] + jnp.where(away == o, used, 0.0) for o in range(WIDE)]
        counts.append(live)
    after = {"lon": lax.rem(lon + 1, lon_count)}
    before = {"lon": lax.rem(lon + lon_count - 1, lon_count)}

    def partner(axis, me, bit):
        low = lax.rem(me // bit, 2)
        return {axis: me + bit - 2 * bit * low}, low

    stages = []
    for axis, me, count in (("dp", dp, dp_count), ("lon", lon, 1 if line else lon_count)):
        bit = 1
        while bit < count:
            stages.append(partner(axis, me, bit))
            bit *= 2
    gathers = []
    held = [0]
    bit = head_count // 2
    while bit:
        for at in list(held):
            gathers.append((bit, at))
            held.append(at + bit)
        bit //= 2

    greeted = [after, before] + [there for there, _ in stages]
    across = partner("lon", lon, 2)[0]
    if line:
        greeted.append(across)
    bit = head_count // 2
    while bit:
        greeted.append(partner("head", head, bit)[0])
        bit //= 2
    barrier = pltpu.get_barrier_semaphore()
    for there in greeted:
        pl.semaphore_signal(barrier, inc=1, device_id=there, device_id_type=MESH)
    pl.semaphore_wait(barrier, len(greeted))

    def remote(src, dst, ss, rs, there):
        return pltpu.make_async_remote_copy(
            src_ref=src, dst_ref=dst, send_sem=ss, recv_sem=rs, device_id=there, device_id_type=MESH
        )

    def piece_at(offset):
        at = 0
        bit = 1
        while bit < head_count:
            low = lax.rem(head // bit, 2)
            at = at + bit * ((1 - low) if offset & bit else low)
            bit *= 2
        return pl.ds(pl.multiple_of(at * piece, piece), piece)

    kv_copies = []
    d_copies = []
    for c in range(chunks):
        cut = slice(c * cols, (c + 1) * cols)
        some, others = [], []
        for n, ref in ((0, k_ref), (1, v_ref)):
            for way, there in ((0, after), (1, before)):
                at = (c * 2 + n) * 2 + way
                some.append(
                    remote(
                        ref.at[:, cut], kv_in.at[way, n, :, cut], kv_ss.at[at], kv_rs.at[at], there
                    )
                )
            for way, there in ((0, before), (1, after)):
                at = (c * 2 + n) * 2 + way
                others.append(
                    remote(
                        dsend.at[way, n, :, cut],
                        drecv.at[way, n, :, cut],
                        d_ss.at[at],
                        d_rs.at[at],
                        there,
                    )
                )
        kv_copies.append(some)
        d_copies.append(others)

    og_copies = []
    for at, (bit, offset) in enumerate(gathers):
        src = og_ref if offset == 0 else og_s.at[piece_at(offset)]
        og_copies.append(
            remote(
                src,
                og_s.at[piece_at(offset)],
                og_ss.at[at],
                og_rs.at[at],
                partner("head", head, bit)[0],
            )
        )

    def each_kv(c, act):
        for at, copy in enumerate(kv_copies[c]):
            if line:
                pl.when(lon != (3 if at % 2 == 0 else 0))(functools.partial(act, copy))
            else:
                act(copy)

    def relay(c, n, way):
        cut = slice(c * cols, (c + 1) * cols)
        return remote(
            kv_in.at[way, n, :, cut],
            kv_in.at[1 - way, n, :, cut],
            relay_ss.at[c * 2 + n],
            kv_rs.at[(c * 2 + n) * 2 + 1 - way],
            across,
        )

    def pass_on(c):
        if not line:
            return
        for way in range(2):

            @pl.when(lon == 1 + way)
            def _():
                for n in range(2):
                    kv_copies[c][n * 2 + way].wait_recv()
                    relay(c, n, way).start()

    def take(c):
        for at, copy in enumerate(kv_copies[c]):
            if line:
                pl.when(lon != 1 + at % 2)(copy.wait_recv)
            else:
                copy.wait_recv()

    each_kv(0, lambda copy: copy.start())
    for copy, (bit, offset) in zip(og_copies, gathers):
        if offset == 0:
            copy.start()
    for c in range(1, chunks - 1):
        each_kv(c, lambda copy: copy.start())
    local_copies = [
        pltpu.make_async_copy(src, dst, local_sem.at[at])
        for at, (src, dst) in enumerate(
            (
                (og_ref, og_s.at[piece_at(0)]),
                (w_ref, w_s),
                (q_ref, q_s),
                (k_ref, k_s),
                (v_ref, v_s),
            )
        )
    ]
    for copy in local_copies:
        copy.start()
    where = {}
    for at, (bit, offset) in enumerate(gathers):
        where[bit + offset] = at
    arrived = set()
    for copy, (bit, offset) in zip(og_copies, gathers):
        if offset:
            og_copies[where[offset]].wait_recv()
            arrived.add(where[offset])
            copy.start()
    pass_on(0)
    each_kv(chunks - 1, lambda copy: copy.start())
    for at, copy in enumerate(og_copies):
        if at not in arrived:
            copy.wait_recv()
    for copy in local_copies:
        copy.wait()

    @pl.loop(0, chunks)
    def _(c):
        ga[:, columns(c * cols, cols)] = mul(
            og_s[...], w_s[pl.ds(pl.multiple_of(c * cols, cols), cols)], NT
        ).astype(jnp.bfloat16)

    @pl.loop(0, model // BLOCK)
    def _(b):
        og_t[pl.ds(pl.multiple_of(b * BLOCK, BLOCK), BLOCK)] = og_s[:, columns(b * BLOCK, BLOCK)].T

    shares = lon_count * dp_count
    share = model // shares
    last = len(stages)
    sent_counts = [shares >> (s + 1) for s in range(last)]
    starts = [sum(sent_counts[:s]) for s in range(last)]

    def weight_copy(s, c):
        span = pl.ds(starts[s], sent_counts[s])
        at = c * last + s
        return remote(
            wsend.at[c, span], wrecv.at[c, span], w_ss.at[at], w_rs.at[at], stages[s][0]
        )

    def share_rows(b):
        return pl.ds(pl.multiple_of(b * share, 16), share)

    def stage(s, c):
        if s > 0:
            weight_copy(s - 1, c).wait_recv()

            @pl.loop(0, sent_counts[s - 1])
            def _(j):
                acc[c, j] += wrecv[c, starts[s - 1] + j].astype(jnp.float32)

        if s == last and not line:
            gw_ref[:, c * cols : (c + 1) * cols] = acc[c, 0]
            return
        if s == last:
            return
        mine = stages[s][1]

        @pl.loop(0, sent_counts[s])
        def _(j):
            if s == 0:
                gone = gw_s[share_rows(2 * j + 1 - mine)]
                kept = gw_s[share_rows(2 * j + mine)]
            else:
                gone = acc[c, 2 * j + 1 - mine]
                kept = acc[c, 2 * j + mine]
            wsend[c, starts[s] + j] = gone.astype(jnp.bfloat16)
            acc[c, j] = kept

        weight_copy(s, c).start()

    def link(c, t, side):
        at = c * 4 + t
        return remote(
            lsend.at[c, t],
            lrecv.at[c, side, t],
            l_ss.at[at],
            l_rs.at[(c * 2 + side) * 4 + t],
            before if side else after,
        )

    def hop(c, t, side, add):
        total = acc[c, t]
        if add:
            link(c, t, side).wait_recv()
            total = total + lrecv[c, side, t].astype(jnp.float32)
        lsend[c, t] = total.astype(jnp.bfloat16)
        link(c, t, side).start()

    def chain(step, c):
        if step == 0:

            @pl.when(lon == 0)
            def _():
                for t in (3, 2, 1):
                    hop(c, t, 0, False)

            @pl.when(lon == 3)
            def _():
                for t in (0, 1, 2):
                    hop(c, t, 1, False)

        elif step == 1:

            @pl.when(lon == 1)
            def _():
                for t in (3, 2):
                    hop(c, t, 0, True)

            @pl.when(lon == 2)
            def _():
                for t in (0, 1):
                    hop(c, t, 1, True)

        elif step == 2:

            @pl.when(lon == 2)
            def _():
                hop(c, 3, 0, True)

            @pl.when(lon == 1)
            def _():
                hop(c, 0, 1, True)

        else:
            for t in range(4):

                @pl.when(lon == t)
                def _():
                    total = acc[c, t]
                    for side, fits in ((0, t > 0), (1, t < 3)):
                        if fits:
                            link(c, t, side).wait_recv()
                            total = total + lrecv[c, side, t].astype(jnp.float32)
                    gw_ref[:, c * cols : (c + 1) * cols] = total

    refs = (q_s, k_s, v_s, ga, kv_in, dq_ref, att_s, own, dsend, ext)
    for c in range(chunks):
        if c + 1 < chunks:
            pass_on(c + 1)
        take(c)

        @pl.loop(0, CHUNK_HEADS)
        def _(h):
            attend_head(c * cols + h * HEAD_DIM, h * HEAD_DIM, counts, refs)

        for copy in d_copies[c]:
            copy.start()

        @pl.loop(0, model // BLOCK)
        def _(b):
            span = pl.ds(pl.multiple_of(b * BLOCK, BLOCK), BLOCK)
            gw_s[span] = mul(og_t[span], att_s[...], NN)

        stage(0, c)
        if c > 0:
            stage(1, c - 1)
            if line:
                chain(0, c - 1)
    stage(1, chunks - 1)

    def join(c):
        cut = slice(c * cols, (c + 1) * cols)
        for copy in d_copies[c]:
            copy.wait_recv()
        for n, ref in ((0, dk_ref), (1, dv_ref)):
            ref[:, cut] = (
                own[n, :, cut]
                + drecv[0, n, :, cut].astype(jnp.float32)
                + drecv[1, n, :, cut].astype(jnp.float32)
            ).astype(jnp.bfloat16)

    if line:
        chain(0, chunks - 1)
        for c in range(chunks):
            chain(1, c)
        for c in range(chunks):
            join(c)
            chain(2, c)
        for c in range(chunks):
            chain(3, c)
    else:
        for s in range(2, last + 1):
            for c in range(chunks):
                stage(s, c)
        for c in range(chunks):
            join(c)
    for copy in og_copies:
        copy.wait_send()
    for c in range(chunks):
        each_kv(c, lambda copy: copy.wait_send())
        if line:
            for way in range(2):

                @pl.when(lon == 1 + way)
                def _():
                    for n in range(2):
                        relay(c, n, way).wait_send()

        for copy in d_copies[c]:
            copy.wait_send()
        for s in range(last):
            weight_copy(s, c).wait_send()
        if line:
            for t in range(4):
                pl.when(lon < t)(link(c, t, 0).wait_send)
                pl.when(lon > t)(link(c, t, 1).wait_send)


def local(queries, key_heads, value_heads, out_grad, out_weight, neighbours, slot_valid):
    q, k, v = queries[0], key_heads[0], value_heads[0]
    rows, features = q.shape
    sizes = tuple(lax.axis_size(axis) for axis in ("lon", "head", "dp"))
    lon_count, head_count, dp_count = sizes
    model = out_weight.shape[1]
    cols = CHUNK_HEADS * HEAD_DIM
    chunks = features // cols
    shares = lon_count * dp_count
    share = model // shares
    bits = shares.bit_length() - 1
    low, wide = jnp.bfloat16, jnp.float32
    vmem = pltpu.VMEM
    dma = pltpu.SemaphoreType.DMA
    dq, dk, dv, gw = pl.pallas_call(
        functools.partial(kernel, sizes),
        out_shape=[
            jax.ShapeDtypeStruct((rows, features), low),
            jax.ShapeDtypeStruct((rows, features), low),
            jax.ShapeDtypeStruct((rows, features), low),
            jax.ShapeDtypeStruct((share, features), wide),
        ],
        in_specs=[pl.BlockSpec(memory_space=pltpu.SMEM)] * 2
        + [pl.BlockSpec(memory_space=pl.ANY)] * 5,
        out_specs=[pl.BlockSpec(memory_space=vmem)] * 4,
        scratch_shapes=[
            vmem((rows, features), low),
            vmem((rows, features), low),
            vmem((rows, features), low),
            vmem((features, model), low),
            vmem((rows, model), low),
            vmem((model, rows), low),
            vmem((rows, features), low),
            vmem((2, 2, rows, features), low),
            vmem((2, 3 * rows, HEAD_DIM), wide),
            vmem((2, rows, features), wide),
            vmem((2, 2, rows, features), low),
            vmem((2, 2, rows, features), low),
            vmem((rows, cols), low),
            vmem((model, cols), wide),
            vmem((chunks, shares // 2, share, cols), wide),
            vmem((chunks, shares - 1, share, cols), low),
            vmem((chunks, shares - 1, share, cols), low),
            dma((5,)),
            dma((chunks * 4,)),
            dma((chunks * 4,)),
            dma((head_count - 1,)),
            dma((head_count - 1,)),
            dma((chunks * 4,)),
            dma((chunks * 4,)),
            dma((chunks * bits,)),
            dma((chunks * bits,)),
            dma((chunks * 2,)),
            vmem((chunks, 4, share, cols), low),
            vmem((chunks, 2, 4, share, cols), low),
            dma((chunks * 4,)),
            dma((chunks * 8,)),
        ],
        compiler_params=pltpu.CompilerParams(
            collective_id=0, has_side_effects=True, vmem_limit_bytes=60 * 1024 * 1024
        ),
    )(neighbours, slot_valid, q, k, v, out_grad[0], out_weight)
    return (dq[None], dk[None], dv[None], gw)


def solution(mesh):
    in_specs = (
        P("dp", "lon", "head"),
        P("dp", "lon", "head"),
        P("dp", "lon", "head"),
        P("dp", ("lon", "head"), None),
        P("head", None),
        P(),
        P(),
    )
    out_specs = (
        P("dp", "lon", "head"),
        P("dp", "lon", "head"),
        P("dp", "lon", "head"),
        P(("lon", "dp"), "head"),
    )
    return jax.shard_map(local, mesh=mesh, in_specs=in_specs, out_specs=out_specs, check_vma=False)
```

```python
import functools
import math

import jax
import jax.numpy as jnp
from jax import lax
from jax.experimental import pallas as pl
from jax.experimental.pallas import tpu as pltpu
from jax.sharding import PartitionSpec as P

HEAD_DIM = 128
TILE = 256
REACH = 2
WIDE = 2 * REACH + 1
CHUNK_HEADS = 2
BLOCK = 256
NT = (((1,), (1,)), ((), ()))
NN = (((1,), (0,)), ((), ()))
TN = (((0,), (0,)), ((), ()))
MESH = pl.DeviceIdType.MESH


def mul(a, b, dims):
    return lax.dot_general(a, b, dims, preferred_element_type=jnp.float32)


def columns(start, size):
    return pl.ds(pl.multiple_of(start, HEAD_DIM), size)


def attend_head(col, att_col, counts, refs):
    factor = 1.0 / math.sqrt(HEAD_DIM)
    q_s, k_s, v_s, ga, kv_in, dq_ref, att_s, own, dsend, ext = refs
    rows = q_s.shape[0]
    tiles = rows // TILE
    lanes = columns(col, HEAD_DIM)

    def tile_of(n, j):
        part, at = divmod(j, tiles)
        here = slice(at * TILE, (at + 1) * TILE)
        if part == 1:
            return (k_s, v_s)[n][here, lanes]
        return kv_in[part // 2, n, here, lanes]

    seen = set()
    for i in range(tiles):
        here = slice(i * TILE, (i + 1) * TILE)
        q = q_s[here, lanes]
        g = ga[here, lanes]
        spots = [i + tiles - REACH + o for o in range(WIDE)]
        live = counts[i]
        scores = []
        top = None
        for o in range(WIDE):
            bias = jnp.where(live[o] > 0.0, 0.0, -jnp.inf)
            s = mul(tile_of(0, spots[o]), q, NT) * factor + bias
            scores.append(s)
            m = jnp.max(s, axis=0, keepdims=True)
            top = m if top is None else jnp.maximum(top, m)
        total = None
        raised = []
        for o in range(WIDE):
            e = jnp.exp(scores[o] - top)
            raised.append(e)
            part = jnp.sum(e, axis=0, keepdims=True) * live[o]
            total = part if total is None else total + part
        inverse = 1.0 / total
        weights = []
        att = None
        for o in range(WIDE):
            w = raised[o] * inverse
            weights.append(w)
            low = w.astype(jnp.bfloat16)
            part = mul(tile_of(1, spots[o]), low, TN) * live[o]
            att = part if att is None else att + part
            dv = mul(low, g, NN) * live[o]
            spot = slice(spots[o] * TILE, (spots[o] + 1) * TILE)
            if spots[o] in seen:
                ext[1, spot] += dv
            else:
                ext[1, spot] = dv
        att_s[here, columns(att_col, HEAD_DIM)] = att.T.astype(jnp.bfloat16)
        g_turned = g.astype(jnp.float32).T
        delta = jnp.sum(
            g_turned * att.astype(jnp.bfloat16).astype(jnp.float32), axis=0, keepdims=True
        )
        dq = None
        for o in range(WIDE):
            dw = mul(tile_of(1, spots[o]), g, NT)
            ds = (weights[o] * (dw - delta) * factor).astype(jnp.bfloat16)
            part = mul(tile_of(0, spots[o]), ds, TN) * live[o]
            dq = part if dq is None else dq + part
            dk = mul(ds, q, NN) * live[o]
            spot = slice(spots[o] * TILE, (spots[o] + 1) * TILE)
            if spots[o] in seen:
                ext[0, spot] += dk
            else:
                ext[0, spot] = dk
            seen.add(spots[o])
        dq_ref[here, lanes] = dq.T.astype(jnp.bfloat16)
    for n in range(2):
        dsend[0, n, :, lanes] = ext[n, 0:rows].astype(jnp.bfloat16)
        own[n, :, lanes] = ext[n, rows : 2 * rows]
        dsend[1, n, :, lanes] = ext[n, 2 * rows : 3 * rows].astype(jnp.bfloat16)


def kernel(
    sizes,
    slots_ref,
    q_ref,
    k_ref,
    v_ref,
    og_ref,
    w_ref,
    grads_ref,
    gw_ref,
    q_s,
    k_s,
    v_s,
    w_s,
    og_s,
    og_t,
    ga,
    kv_in,
    ext,
    own,
    dsend,
    drecv,
    att_s,
    gw_s,
    acc,
    wsend,
    wrecv,
    local_sem,
    kv_ss,
    kv_rs,
    og_ss,
    og_rs,
    d_ss,
    d_rs,
    w_ss,
    w_rs,
    relay_ss,
    lsend,
    lrecv,
    l_ss,
    l_rs,
):
    lon_count, head_count, dp_count = sizes
    dq_ref, dk_ref, dv_ref = (grads_ref.at[n] for n in range(3))
    rows, features = q_s.shape
    model = og_s.shape[1]
    piece = og_ref.shape[0]
    cols = CHUNK_HEADS * HEAD_DIM
    chunks = features // cols
    lon = lax.axis_index("lon")
    head = lax.axis_index("head")
    dp = lax.axis_index("dp")
    line = lon_count == 4
    tiles = rows // TILE
    counts = []
    for i in range(tiles):
        tile = lon * tiles + i
        live = [jnp.float32(1.0 if o == REACH else 0.0) for o in range(WIDE)]
        for j in range(slots_ref.shape[0]):
            slot = slots_ref[j, tile]
            away = lax.rem(slot // 2 - tile + REACH + tiles * lon_count, tiles * lon_count)
            used = jnp.where(lax.rem(slot, 2) > 0, 1.0, 0.0)
            live = [live[o] + jnp.where(away == o, used, 0.0) for o in range(WIDE)]
        counts.append(live)
    after = {"lon": lax.rem(lon + 1, lon_count)}
    before = {"lon": lax.rem(lon + lon_count - 1, lon_count)}

    def partner(axis, me, bit):
        low = lax.rem(me // bit, 2)
        return {axis: me + bit - 2 * bit * low}, low

    stages = []
    for axis, me, count in (("dp", dp, dp_count), ("lon", lon, 1 if line else lon_count)):
        bit = 1
        while bit < count:
            stages.append(partner(axis, me, bit))
            bit *= 2
    gathers = []
    held = [0]
    bit = head_count // 2
    while bit:
        for at in list(held):
            gathers.append((bit, at))
            held.append(at + bit)
        bit //= 2

    greeted = [after, before] + [there for there, _ in stages]
    across = partner("lon", lon, 2)[0]
    if line:
        greeted.append(across)
    bit = head_count // 2
    while bit:
        greeted.append(partner("head", head, bit)[0])
        bit //= 2
    barrier = pltpu.get_barrier_semaphore()
    for there in greeted:
        pl.semaphore_signal(barrier, inc=1, device_id=there, device_id_type=MESH)
    pl.semaphore_wait(barrier, len(greeted))

    def remote(src, dst, ss, rs, there):
        return pltpu.make_async_remote_copy(
            src_ref=src, dst_ref=dst, send_sem=ss, recv_sem=rs, device_id=there, device_id_type=MESH
        )

    def piece_at(offset):
        at = 0
        bit = 1
        while bit < head_count:
            low = lax.rem(head // bit, 2)
            at = at + bit * ((1 - low) if offset & bit else low)
            bit *= 2
        return pl.ds(pl.multiple_of(at * piece, piece), piece)

    kv_copies = []
    d_copies = []
    for c in range(chunks):
        cut = slice(c * cols, (c + 1) * cols)
        some, others = [], []
        for n, ref in ((0, k_ref), (1, v_ref)):
            for way, there in ((0, after), (1, before)):
                at = (c * 2 + n) * 2 + way
                some.append(
                    remote(
                        ref.at[:, cut], kv_in.at[way, n, :, cut], kv_ss.at[at], kv_rs.at[at], there
                    )
                )
            for way, there in ((0, before), (1, after)):
                at = (c * 2 + n) * 2 + way
                others.append(
                    remote(
                        dsend.at[way, n, :, cut],
                        drecv.at[way, n, :, cut],
                        d_ss.at[at],
                        d_rs.at[at],
                        there,
                    )
                )
        kv_copies.append(some)
        d_copies.append(others)

    og_copies = []
    for at, (bit, offset) in enumerate(gathers):
        src = og_ref if offset == 0 else og_s.at[piece_at(offset)]
        og_copies.append(
            remote(
                src,
                og_s.at[piece_at(offset)],
                og_ss.at[at],
                og_rs.at[at],
                partner("head", head, bit)[0],
            )
        )

    def each_kv(c, act):
        for at, copy in enumerate(kv_copies[c]):
            if line:
                pl.when(lon != (3 if at % 2 == 0 else 0))(functools.partial(act, copy))
            else:
                act(copy)

    def relay(c, n, way):
        cut = slice(c * cols, (c + 1) * cols)
        return remote(
            kv_in.at[way, n, :, cut],
            kv_in.at[1 - way, n, :, cut],
            relay_ss.at[c * 2 + n],
            kv_rs.at[(c * 2 + n) * 2 + 1 - way],
            across,
        )

    def pass_on(c):
        if not line:
            return
        for way in range(2):

            @pl.when(lon == 1 + way)
            def _():
                for n in range(2):
                    kv_copies[c][n * 2 + way].wait_recv()
                    relay(c, n, way).start()

    def take(c):
        for at, copy in enumerate(kv_copies[c]):
            if line:
                pl.when(lon != 1 + at % 2)(copy.wait_recv)
            else:
                copy.wait_recv()

    each_kv(0, lambda copy: copy.start())
    for copy, (bit, offset) in zip(og_copies, gathers):
        if offset == 0:
            copy.start()
    for c in range(1, chunks - 1):
        each_kv(c, lambda copy: copy.start())
    local_copies = [
        pltpu.make_async_copy(src, dst, local_sem.at[at])
        for at, (src, dst) in enumerate(
            (
                (og_ref, og_s.at[piece_at(0)]),
                (w_ref, w_s),
                (q_ref, q_s),
                (k_ref, k_s),
                (v_ref, v_s),
            )
        )
    ]
    for copy in local_copies:
        copy.start()
    where = {}
    for at, (bit, offset) in enumerate(gathers):
        where[bit + offset] = at
    arrived = set()
    for copy, (bit, offset) in zip(og_copies, gathers):
        if offset:
            og_copies[where[offset]].wait_recv()
            arrived.add(where[offset])
            copy.start()
    pass_on(0)
    each_kv(chunks - 1, lambda copy: copy.start())
    for at, copy in enumerate(og_copies):
        if at not in arrived:
            copy.wait_recv()
    for copy in local_copies:
        copy.wait()

    @pl.loop(0, chunks)
    def _(c):
        ga[:, columns(c * cols, cols)] = mul(
            og_s[...], w_s[pl.ds(pl.multiple_of(c * cols, cols), cols)], NT
        ).astype(jnp.bfloat16)

    @pl.loop(0, model // BLOCK)
    def _(b):
        og_t[pl.ds(pl.multiple_of(b * BLOCK, BLOCK), BLOCK)] = og_s[:, columns(b * BLOCK, BLOCK)].T

    shares = lon_count * dp_count
    share = model // shares
    last = len(stages)
    sent_counts = [shares >> (s + 1) for s in range(last)]
    starts = [sum(sent_counts[:s]) for s in range(last)]

    def weight_copy(s, c):
        span = pl.ds(starts[s], sent_counts[s])
        at = c * last + s
        return remote(
            wsend.at[c, span], wrecv.at[c, span], w_ss.at[at], w_rs.at[at], stages[s][0]
        )

    def share_rows(b):
        return pl.ds(pl.multiple_of(b * share, 16), share)

    def stage(s, c):
        if s > 0:
            weight_copy(s - 1, c).wait_recv()

            @pl.loop(0, sent_counts[s - 1])
            def _(j):
                acc[c, j] += wrecv[c, starts[s - 1] + j].astype(jnp.float32)

        if s == last and not line:
            gw_ref[:, c * cols : (c + 1) * cols] = acc[c, 0]
            return
        if s == last:
            return
        mine = stages[s][1]

        @pl.loop(0, sent_counts[s])
        def _(j):
            if s == 0:
                gone = gw_s[share_rows(2 * j + 1 - mine)]
                kept = gw_s[share_rows(2 * j + mine)]
            else:
                gone = acc[c, 2 * j + 1 - mine]
                kept = acc[c, 2 * j + mine]
            wsend[c, starts[s] + j] = gone.astype(jnp.bfloat16)
            acc[c, j] = kept

        weight_copy(s, c).start()

    def link(c, t, side):
        at = c * 4 + t
        return remote(
            lsend.at[c, t],
            lrecv.at[c, side, t],
            l_ss.at[at],
            l_rs.at[(c * 2 + side) * 4 + t],
            before if side else after,
        )

    def hop(c, t, side, add):
        total = acc[c, t]
        if add:
            link(c, t, side).wait_recv()
            total = total + lrecv[c, side, t].astype(jnp.float32)
        lsend[c, t] = total.astype(jnp.bfloat16)
        link(c, t, side).start()

    def chain(step, c):
        if step == 0:

            @pl.when(lon == 0)
            def _():
                for t in (3, 2, 1):
                    hop(c, t, 0, False)

            @pl.when(lon == 3)
            def _():
                for t in (0, 1, 2):
                    hop(c, t, 1, False)

        elif step == 1:

            @pl.when(lon == 1)
            def _():
                for t in (3, 2):
                    hop(c, t, 0, True)

            @pl.when(lon == 2)
            def _():
                for t in (0, 1):
                    hop(c, t, 1, True)

        elif step == 2:

            @pl.when(lon == 2)
            def _():
                hop(c, 3, 0, True)

            @pl.when(lon == 1)
            def _():
                hop(c, 0, 1, True)

        else:
            for t in range(4):

                @pl.when(lon == t)
                def _():
                    total = acc[c, t]
                    for side, fits in ((0, t > 0), (1, t < 3)):
                        if fits:
                            link(c, t, side).wait_recv()
                            total = total + lrecv[c, side, t].astype(jnp.float32)
                    gw_ref[:, c * cols : (c + 1) * cols] = total

    refs = (q_s, k_s, v_s, ga, kv_in, dq_ref, att_s, own, dsend, ext)
    for c in range(chunks):
        if c + 1 < chunks:
            pass_on(c + 1)
        take(c)

        @pl.loop(0, CHUNK_HEADS)
        def _(h):
            attend_head(c * cols + h * HEAD_DIM, h * HEAD_DIM, counts, refs)

        for copy in d_copies[c]:
            copy.start()

        @pl.loop(0, model // BLOCK)
        def _(b):
            span = pl.ds(pl.multiple_of(b * BLOCK, BLOCK), BLOCK)
            gw_s[span] = mul(og_t[span], att_s[...], NN)

        stage(0, c)
        if c > 0:
            stage(1, c - 1)
            if line:
                chain(0, c - 1)
    stage(1, chunks - 1)

    def join(c):
        cut = slice(c * cols, (c + 1) * cols)
        for copy in d_copies[c]:
            copy.wait_recv()
        for n, ref in ((0, dk_ref), (1, dv_ref)):
            ref[:, cut] = (
                own[n, :, cut]
                + drecv[0, n, :, cut].astype(jnp.float32)
                + drecv[1, n, :, cut].astype(jnp.float32)
            ).astype(jnp.bfloat16)

    if line:
        chain(0, chunks - 1)
        for c in range(chunks):
            chain(1, c)
        for c in range(chunks):
            join(c)
            chain(2, c)
        for c in range(chunks):
            chain(3, c)
    else:
        for s in range(2, last + 1):
            for c in range(chunks):
                stage(s, c)
        for c in range(chunks):
            join(c)
    for copy in og_copies:
        copy.wait_send()
    for c in range(chunks):
        each_kv(c, lambda copy: copy.wait_send())
        if line:
            for way in range(2):

                @pl.when(lon == 1 + way)
                def _():
                    for n in range(2):
                        relay(c, n, way).wait_send()

        for copy in d_copies[c]:
            copy.wait_send()
        for s in range(last):
            weight_copy(s, c).wait_send()
        if line:
            for t in range(4):
                pl.when(lon < t)(link(c, t, 0).wait_send)
                pl.when(lon > t)(link(c, t, 1).wait_send)


def local(queries, key_heads, value_heads, out_grad, out_weight, neighbours, slot_valid):
    q, k, v = queries[0], key_heads[0], value_heads[0]
    rows, features = q.shape
    sizes = tuple(lax.axis_size(axis) for axis in ("lon", "head", "dp"))
    lon_count, head_count, dp_count = sizes
    model = out_weight.shape[1]
    cols = CHUNK_HEADS * HEAD_DIM
    chunks = features // cols
    shares = lon_count * dp_count
    share = model // shares
    bits = shares.bit_length() - 1
    low, wide = jnp.bfloat16, jnp.float32
    vmem = pltpu.VMEM
    dma = pltpu.SemaphoreType.DMA
    slots = neighbours.T * 2 + (slot_valid.T > 0).astype(jnp.int32)
    grads, gw = pl.pallas_call(
        functools.partial(kernel, sizes),
        out_shape=[
            jax.ShapeDtypeStruct((3, rows, features), low),
            jax.ShapeDtypeStruct((share, features), wide),
        ],
        in_specs=[pl.BlockSpec(memory_space=pltpu.SMEM)]
        + [pl.BlockSpec(memory_space=pl.ANY)] * 5,
        out_specs=[pl.BlockSpec(memory_space=vmem)] * 2,
        scratch_shapes=[
            vmem((rows, features), low),
            vmem((rows, features), low),
            vmem((rows, features), low),
            vmem((features, model), low),
            vmem((rows, model), low),
            vmem((model, rows), low),
            vmem((rows, features), low),
            vmem((2, 2, rows, features), low),
            vmem((2, 3 * rows, HEAD_DIM), wide),
            vmem((2, rows, features), wide),
            vmem((2, 2, rows, features), low),
            vmem((2, 2, rows, features), low),
            vmem((rows, cols), low),
            vmem((model, cols), wide),
            vmem((chunks, shares // 2, share, cols), wide),
            vmem((chunks, shares - 1, share, cols), low),
            vmem((chunks, shares - 1, share, cols), low),
            dma((5,)),
            dma((chunks * 4,)),
            dma((chunks * 4,)),
            dma((head_count - 1,)),
            dma((head_count - 1,)),
            dma((chunks * 4,)),
            dma((chunks * 4,)),
            dma((chunks * bits,)),
            dma((chunks * bits,)),
            dma((chunks * 2,)),
            vmem((chunks, 4, share, cols), low),
            vmem((chunks, 2, 4, share, cols), low),
            dma((chunks * 4,)),
            dma((chunks * 8,)),
        ],
        compiler_params=pltpu.CompilerParams(
            collective_id=0, has_side_effects=True, vmem_limit_bytes=60 * 1024 * 1024
        ),
    )(slots, q, k, v, out_grad[0], out_weight)
    return (grads[0][None], grads[1][None], grads[2][None], gw)


def solution(mesh):
    in_specs = (
        P("dp", "lon", "head"),
        P("dp", "lon", "head"),
        P("dp", "lon", "head"),
        P("dp", ("lon", "head"), None),
        P("head", None),
        P(),
        P(),
    )
    out_specs = (
        P("dp", "lon", "head"),
        P("dp", "lon", "head"),
        P("dp", "lon", "head"),
        P(("lon", "dp"), "head"),
    )
    return jax.shard_map(local, mesh=mesh, in_specs=in_specs, out_specs=out_specs, check_vma=False)
```
